32 devices in a mesh: row: 8 (over z, x), col: 4 (over y, core).
Axes of the slice: x: 2, y: 2, z: 4, core: 2. Of those that a mesh axis runs over, the one named last changes fastest.
Arguments:
- tmatrix: bfloat16 [10656, 10656], P('row', 'col'), may hold values from -0.0625 to 0.0625
- panel: bfloat16 [10656, 2048], P('col', 'row'), may hold values from -6 to 6
- contrast: float32 [3, 144, 288], replicated, may hold values from -1.5 to 1.5
Outputs:
- excitation: bfloat16 [10656, 2048], P('col', 'row')
The draws below stay inside these ranges and needn't reach their ends.
All inputs are finite; a program needn't handle non-finite values.
Results may differ from the reference program's by a relative error of at most 0.006.
Values may be sent and summed in bfloat16 or wider, within the bound.
No kernel may reach another device: no remote copies, remote signals or barrier semaphores. Data moves between devices by JAX's collectives and lax.ppermute only.
A program may use at most 192 MiB of HBM per device.

```python
import jax
import jax.numpy as jnp
import numpy as np
from jax import lax

LDEG = 72
ORDER = 10656
NT = 144
NP = 288
PANEL = 2048
ITERS = 2
N_COL = 4


def level_of(stream_key, dims, pieces, low, largest):
    loudness = 1.0
    for position, blocks in pieces:
        steps = jax.random.uniform(jax.random.fold_in(jax.random.fold_in(stream_key, 6), position), (blocks,), jnp.float32, low / len(pieces), largest / len(pieces))
        loudness = loudness * jnp.repeat(jnp.exp(steps), dims[position] // blocks).reshape((-1,) + (1,) * (len(dims) - 1 - position))
    return loudness


def noise(stream_key, dims, spread, most, pieces=(), kind=jnp.bfloat16):
    values = spread * jax.random.normal(stream_key, dims, jnp.float32)
    if pieces:
        values = values * level_of(stream_key, dims, pieces, -0.22, 0.18)
    return jnp.clip(values, -most, most).astype(kind)


def setup_inputs(seed: int = 0) -> dict:
    key_list = jax.random.split(jax.random.key(seed), 4)
    tmatrix = noise(key_list[0], (ORDER, ORDER), ORDER ** -0.5, 0.0625, ((0, 8), (1, 4)))
    panel = noise(key_list[1], (ORDER, PANEL), 1.0, 6.0, ((0, 4), (1, 8)))
    contrast = noise(key_list[2], (3, NT, NP), 0.3, 1.5, (), jnp.float32)
    return {"tmatrix": tmatrix, "panel": panel, "contrast": contrast}


def angular_tables(degree):
    lat_count = 2 * degree
    lon_count = 4 * degree
    freq_count = 2 * degree + 1
    colatitude = (np.arange(lat_count) + 0.5) * np.pi / lat_count
    cos_col = np.cos(colatitude)
    sin_col = np.sin(colatitude)
    legendre = np.zeros((freq_count, degree, lat_count))
    diagonal_term = np.full(lat_count, np.sqrt(0.5))
    for order_m in range(degree + 1):
        if order_m > 0:
            diagonal_term = diagonal_term * np.sqrt((2.0 * order_m + 1.0) / (2.0 * order_m)) * sin_col
        earlier = np.zeros(lat_count)
        latest = diagonal_term
        for degree_l in range(order_m, degree + 1):
            if degree_l == order_m:
                current = diagonal_term
            elif degree_l == order_m + 1:
                current = np.sqrt(2.0 * order_m + 3.0) * cos_col * diagonal_term
            else:
                factor_a = np.sqrt((4.0 * degree_l ** 2 - 1.0) / (degree_l ** 2 - order_m ** 2))
                factor_b = np.sqrt(((degree_l - 1.0) ** 2 - order_m ** 2) / (4.0 * (degree_l - 1.0) ** 2 - 1.0))
                current = factor_a * (cos_col * latest - factor_b * earlier)
            if degree_l > order_m:
                earlier, latest = (latest, current)
            if degree_l >= 1:
                legendre[order_m, degree_l - 1] = current
                if order_m >= 1:
                    legendre[degree + order_m, degree_l - 1] = current
    longitude = 2.0 * np.pi * np.arange(lon_count) / lon_count
    fourier = np.zeros((freq_count, lon_count))
    fourier[0] = 1.0 / np.sqrt(2.0 * np.pi)
    for order_m in range(1, degree + 1):
        fourier[order_m] = np.cos(order_m * longitude) / np.sqrt(np.pi)
        fourier[degree + order_m] = np.sin(order_m * longitude) / np.sqrt(np.pi)
    weight = sin_col * (np.pi / lat_count) * (2.0 * np.pi / lon_count)
    flat_list = []
    for freq_index in range(freq_count):
        order_m = freq_index if freq_index <= degree else freq_index - degree
        for level_index in range(degree):
            if level_index + 1 >= order_m:
                flat_list.append(freq_index * degree + level_index)
    flat_index = np.array(flat_list, dtype=np.int32)
    return (legendre, fourier, weight, flat_index)

def contrast_apply(coefficients, contrast, degree):
    legendre, fourier, weight, flat_index = angular_tables(degree)
    legendre = jnp.asarray(legendre, jnp.float32)
    fourier = jnp.asarray(fourier, jnp.float32)
    weight = jnp.asarray(weight, jnp.float32)
    freq_count, level_count = (legendre.shape[0], legendre.shape[1])
    columns = coefficients.shape[1]
    halves = coefficients.astype(jnp.float32).reshape(2, -1, columns)
    padded = jnp.zeros((2, freq_count * level_count, columns), jnp.float32).at[:, flat_index, :].set(halves)
    padded = padded.reshape(2, freq_count, level_count, columns)
    highest = lax.Precision.HIGHEST
    latitude = jnp.einsum('qlt,cqlk->cktq', legendre, padded, precision=highest)
    surface = jnp.einsum('cktq,qp->cktp', latitude, fourier, precision=highest)
    polar = contrast[0] * surface[0] + contrast[1] * surface[1]
    azimuth = contrast[1] * surface[0] + contrast[2] * surface[1]
    weighted = jnp.stack([polar, azimuth]) * weight[:, None]
    spectrum = jnp.einsum('cktp,qp->cktq', weighted, fourier, precision=highest)
    projected = jnp.einsum('qlt,cktq->cqlk', legendre, spectrum, precision=highest)
    picked = projected.reshape(2, freq_count * level_count, columns)[:, flat_index, :]
    return picked.reshape(-1, columns).astype(jnp.bfloat16)

def reference(tmatrix, panel, contrast):
    col_block = ORDER // N_COL
    map_width = min(128, PANEL)
    current = panel
    for iteration in range(ITERS):
        summed = jnp.zeros((ORDER, PANEL), jnp.float32)
        for block_index in range(N_COL):
            lower = block_index * col_block
            partial_value = jnp.dot(tmatrix[:, lower:lower + col_block], current[lower:lower + col_block], preferred_element_type=jnp.float32).astype(jnp.bfloat16)
            partial_value = lax.optimization_barrier(partial_value)
            summed = summed + partial_value.astype(jnp.float32)
        scattered = summed.astype(jnp.bfloat16)
        blocks = scattered.reshape(ORDER, PANEL // map_width, map_width).transpose(1, 0, 2)
        mapped = lax.map(lambda column_block: contrast_apply(column_block, contrast, LDEG), blocks)
        coupled = mapped.transpose(1, 0, 2).reshape(ORDER, PANEL)
        current = (panel.astype(jnp.float32) + coupled.astype(jnp.float32)).astype(jnp.bfloat16)
    return current
```

```python
import functools
import jax
import jax.numpy as jnp
import numpy as np
from jax import lax
from jax.experimental import pallas as pl
from jax.experimental.pallas import tpu as pltpu
from jax.sharding import PartitionSpec as P

ITERS = 2

def angular_tables(degree):
    lat_count = 2 * degree
    lon_count = 4 * degree
    colatitude = (np.arange(lat_count) + 0.5) * np.pi / lat_count
    cos_col = np.cos(colatitude)
    sin_col = np.sin(colatitude)
    legendre = np.zeros((degree + 1, degree, lat_count))
    diagonal_term = np.full(lat_count, np.sqrt(0.5))
    for order_m in range(degree + 1):
        if order_m > 0:
            diagonal_term = (
                diagonal_term * np.sqrt((2.0 * order_m + 1.0) / (2.0 * order_m)) * sin_col
            )
        earlier = np.zeros(lat_count)
        latest = diagonal_term
        for degree_l in range(order_m, degree + 1):
            if degree_l == order_m:
                current = diagonal_term
            elif degree_l == order_m + 1:
                current = np.sqrt(2.0 * order_m + 3.0) * cos_col * diagonal_term
            else:
                factor_a = np.sqrt((4.0 * degree_l**2 - 1.0) / (degree_l**2 - order_m**2))
                factor_b = np.sqrt(
                    ((degree_l - 1.0) ** 2 - order_m**2) / (4.0 * (degree_l - 1.0) ** 2 - 1.0)
                )
                current = factor_a * (cos_col * latest - factor_b * earlier)
            if degree_l > order_m:
                earlier, latest = (latest, current)
            if degree_l >= 1:
                legendre[order_m, degree_l - 1] = current
    angle = 2.0 * np.pi * np.arange(lon_count) / lon_count
    cosines = np.cos(np.arange(degree + 1)[:, None] * angle) / np.sqrt(np.pi)
    cosines[0] = 1.0 / np.sqrt(2.0 * np.pi)
    sines = np.sin(np.arange(degree + 1)[:, None] * angle) / np.sqrt(np.pi)
    weight = sin_col * (np.pi / lat_count) * (2.0 * np.pi / lon_count)
    return legendre, cosines, sines, weight


def up(value, unit):
    return -(-value // unit) * unit


def split(table):
    high = table.astype(np.float32).astype(jnp.bfloat16)
    low = (table - high.astype(np.float64)).astype(jnp.bfloat16)
    return high, low


@functools.lru_cache(maxsize=None)
def shell_tables(degree):
    legendre, cosines, sines, weight = angular_tables(degree)
    lat_count, half = 2 * degree, 2 * degree
    slots = up(degree + 1, 16)
    window = up(degree + 7, 16)
    pairs = up(half + 1, 8)
    starts = np.cumsum([0, degree] + [degree + 1 - m for m in range(1, degree + 1)])
    cosine_rows = int(starts[-1])
    sine_shift = -(cosine_rows - degree) % 8
    offsets = np.zeros(slots, np.int32)
    shifted = np.zeros((slots, window, lat_count))
    for m in range(degree + 1):
        offsets[m] = starts[m] // 8 * 8
        first = max(m - 1, 0)
        place = starts[m] - offsets[m]
        shifted[m, place : place + degree - first] = legendre[m, first:]
    high, low = split(shifted)
    synth = np.concatenate([high, low], axis=1).transpose(0, 2, 1)
    analyse = np.concatenate([high, low], axis=1)
    fold = np.zeros((2, slots, pairs))
    fold[0, : degree + 1, : half + 1] = cosines[:, : half + 1]
    fold[1, : degree + 1, 1:half] = sines[:, 1:half]
    fhigh, flow = split(fold)
    inverse = np.concatenate([fhigh, flow], axis=1).transpose(0, 2, 1)
    forward = np.concatenate([fhigh, flow], axis=1)
    return dict(
        slots=slots, window=window, pairs=pairs, cosine_rows=cosine_rows,
        sine_shift=sine_shift, sine_gap=cosine_rows - degree + sine_shift,
        offsets=offsets, synth=np.ascontiguousarray(synth), analyse=analyse,
        inverse=np.ascontiguousarray(inverse), forward=forward, weight=weight,
    )


GROUP = 32


def arrange_contrast(contrast, table):
    comps, lat_count, lon_count = contrast.shape
    half, pairs = lon_count // 2, table["pairs"]
    scaled = contrast * jnp.asarray(table["weight"], jnp.float32)[:, None]
    plus = jnp.pad(scaled[:, :, : half + 1], ((0, 0), (0, 0), (0, pairs - half - 1)))
    minus = jnp.pad(scaled[:, :, half + 1 :][:, :, ::-1], ((0, 0), (0, 0), (1, pairs - half)))
    both = jnp.stack([plus, minus])
    groups = -(-lat_count // GROUP)
    both = jnp.pad(both, ((0, 0), (0, 1), (0, groups * GROUP - lat_count), (0, 0)))
    both = both.reshape(2, comps + 1, groups, GROUP, pairs)
    return both.transpose(2, 0, 4, 3, 1).reshape(groups, 2, pairs, GROUP * (comps + 1))


def shell_kernel(table, unroll, scalar_ref, x_ref, con_ref, synth_ref, analyse_ref, inverse_ref,
                 forward_ref, o_ref, rows_ref, grid_ref):
    slots, window, pairs = table["slots"], table["window"], table["pairs"]
    cosine_rows, gap, shift = table["cosine_rows"], table["sine_gap"], table["sine_shift"]
    lat_count = synth_ref.shape[1]
    pieces, columns, length = x_ref.shape
    full = pieces * length // 2
    lanes = 2 * columns
    f32, bf16 = jnp.float32, jnp.bfloat16

    def place(row):
        return row if row < cosine_rows else row + shift

    cut = cosine_rows // 8 * 8
    rows_ref[cut : cut + 16, :] = jnp.zeros((16, lanes), f32)
    tail = (full + shift) // 8 * 8
    rows_ref[tail:, :] = jnp.zeros((rows_ref.shape[0] - tail, lanes), f32)
    for piece in range(pieces // 2):
        upper = scalar_ref[slots + piece]
        lower = scalar_ref[slots + piece + pieces // 2]
        for start in range(0, length, 128):
            size = min(128, length - start)
            block = jnp.concatenate(
                [x_ref[upper, :, start : start + size], x_ref[lower, :, start : start + size]], axis=0
            ).astype(f32)
            turned = block.T
            base = piece * length + start
            if base < cosine_rows < base + size:
                first = cosine_rows - base
                rows_ref[base : base + first, :] = turned[:first]
                rows_ref[base + first + shift : base + size + shift, :] = turned[first:]
            else:
                rows_ref[place(base) : place(base) + size, :] = turned

    def synthesis(step, carry):
        for inner in range(unroll[0]):
            m = step * unroll[0] + inner
            off = pl.multiple_of(scalar_ref[m], 8)
            both = jnp.concatenate(
                [rows_ref[pl.ds(off, window), :], rows_ref[pl.ds(off + gap, window), :]], axis=1
            ).astype(bf16)
            out = jnp.dot(synth_ref[m], jnp.concatenate([both, both], axis=0), preferred_element_type=f32)
            grid_ref[pl.ds(m, lat_count, stride=2 * slots), :] = out[:, :lanes]
            grid_ref[pl.ds(m + slots, lat_count, stride=2 * slots), :] = out[:, lanes:]
        return carry

    lax.fori_loop(0, slots // unroll[0], synthesis, 0)

    lane = lax.broadcasted_iota(jnp.int32, (pairs, lanes), 1)
    own = jnp.where(lane < columns, 0, 2)

    def longitude(step, carry):
        for inner in range(unroll[1]):
            pair = step * unroll[1] + inner
            base = [pl.multiple_of((2 * pair + j) * 2 * slots, 8) for j in range(2)]
            cos_in = jnp.concatenate([grid_ref[pl.ds(b, slots), :] for b in base], axis=1).astype(bf16)
            sin_in = jnp.concatenate([grid_ref[pl.ds(b + slots, slots), :] for b in base], axis=1).astype(bf16)
            even = jnp.dot(inverse_ref[0], jnp.concatenate([cos_in, cos_in], axis=0), preferred_element_type=f32)
            odd = jnp.dot(inverse_ref[1], jnp.concatenate([sin_in, sin_in], axis=0), preferred_element_type=f32)
            evens, odds = [], []
            for j in range(2):
                t = 2 * pair + j
                part = slice(j * lanes, (j + 1) * lanes)
                lane_base = (t % GROUP) * 4
                vals = []
                for sign in range(2):
                    surface = even[:, part] + odd[:, part] if sign == 0 else even[:, part] - odd[:, part]
                    source = con_ref[t // GROUP, sign]
                    own_c = jnp.take_along_axis(source, own + lane_base, axis=1)
                    cross_c = jnp.take_along_axis(source, jnp.full((pairs, lanes), 1, jnp.int32) + lane_base, axis=1)
                    vals.append(own_c * surface + cross_c * pltpu.roll(surface, columns, 1))
                evens.append(vals[0] + vals[1])
                odds.append(vals[0] - vals[1])
            evens = jnp.concatenate(evens, axis=1).astype(bf16)
            odds = jnp.concatenate(odds, axis=1).astype(bf16)
            back = jnp.dot(forward_ref[0], evens, preferred_element_type=f32)
            back = back[:slots] + back[slots:]
            for j in range(2):
                grid_ref[pl.ds(base[j], slots), :] = back[:, j * lanes : (j + 1) * lanes]
            back = jnp.dot(forward_ref[1], odds, preferred_element_type=f32)
            back = back[:slots] + back[slots:]
            for j in range(2):
                grid_ref[pl.ds(base[j] + slots, slots), :] = back[:, j * lanes : (j + 1) * lanes]
        return carry

    lax.fori_loop(0, lat_count // 2 // unroll[1], longitude, 0)

    rows_ref[...] = jnp.zeros(rows_ref.shape, f32)

    def analysis(step, carry):
        for inner in range(unroll[2]):
            m = step * unroll[2] + inner
            off = pl.multiple_of(scalar_ref[m], 8)
            both = jnp.concatenate(
                [grid_ref[pl.ds(m, lat_count, stride=2 * slots), :],
                 grid_ref[pl.ds(m + slots, lat_count, stride=2 * slots), :]], axis=1
            ).astype(bf16)
            out = jnp.dot(analyse_ref[m], both, preferred_element_type=f32)
            out = out[:window] + out[window:]
            rows_ref[pl.ds(off, window), :] += out[:, :lanes]
            rows_ref[pl.ds(off + gap, window), :] += out[:, lanes:]
        return carry

    lax.fori_loop(0, slots // unroll[2], analysis, 0)

    blocks = o_ref.shape[0]
    mine = scalar_ref[slots + pieces]
    size_out = o_ref.shape[2]
    for block in range(blocks // 2):
        for start in range(0, size_out, 128):
            size = min(128, size_out - start)
            base = block * size_out + start
            if base < cosine_rows < base + size:
                value = jnp.concatenate(
                    [rows_ref[base:cosine_rows, :], rows_ref[cosine_rows + shift : base + size + shift, :]], axis=0
                )
            else:
                value = rows_ref[place(base) : place(base) + size, :]
            turned = value.T.astype(bf16)
            o_ref[block ^ mine, :, start : start + size] = turned[:columns]
            o_ref[(block + blocks // 2) ^ mine, :, start : start + size] = turned[columns:]


def couple(scalars, arrived, arranged, table, blocks, unroll=(4, 1, 4)):
    pieces, columns, length = arrived.shape
    full = pieces * length // 2
    lat_count = table["synth"].shape[1]
    rows = up(int(table["offsets"].max()) + table["sine_gap"] + table["window"], 8)
    vm = pl.BlockSpec(memory_space=pltpu.VMEM)
    return pl.pallas_call(
        functools.partial(shell_kernel, table, unroll),
        out_shape=jax.ShapeDtypeStruct((blocks, columns, pieces * length // blocks), jnp.bfloat16),
        in_specs=[pl.BlockSpec(memory_space=pltpu.SMEM)] + [vm] * 6,
        out_specs=vm,
        scratch_shapes=[
            pltpu.VMEM((rows, 2 * columns), jnp.float32),
            pltpu.VMEM((lat_count * 2 * table["slots"], 2 * columns), jnp.float32),
        ],
        cost_estimate=pl.CostEstimate(
            flops=16 * full * lat_count * 2 * columns, bytes_accessed=16 << 20, transcendentals=0
        ),
        compiler_params=pltpu.CompilerParams(vmem_limit_bytes=60 << 20),
    )(scalars, arrived, arranged, jnp.asarray(table["synth"]), jnp.asarray(table["analyse"]),
      jnp.asarray(table["inverse"]), jnp.asarray(table["forward"]))


def ring_of(mesh):
    count = mesh.devices.shape[0]
    spots = [getattr(d, "coords", None) for d in mesh.devices[:, 0]]
    plain = list(range(count))
    if any(s is None for s in spots):
        return plain
    moving = [a for a in range(len(spots[0])) if len({s[a] for s in spots}) > 1]
    if len(moving) != 2:
        return plain
    sizes = {a: len({s[a] for s in spots}) for a in moving}
    even = sorted((a for a in moving if sizes[a] % 2 == 0), key=lambda a: sizes[a])
    if not even or sizes[moving[0]] * sizes[moving[1]] != count:
        return plain
    outer = even[0]
    inner = moving[0] if moving[1] == outer else moving[1]
    where = {(s[outer], s[inner]): i for i, s in enumerate(spots)}
    first = sorted({s[outer] for s in spots})
    second = sorted({s[inner] for s in spots})
    path = []
    for step, i in enumerate(first):
        path += [(i, j) for j in (second[1:] if step % 2 == 0 else second[:0:-1])]
    path += [(i, second[0]) for i in reversed(first)]
    return [where[p] for p in path]


def body(order, tmatrix, panel, contrast):
    row_count, col_count = lax.axis_size("row"), lax.axis_size("col")
    mine_row, mine_col = lax.axis_index("row"), lax.axis_index("col")
    depth, width = panel.shape
    per_device = width // col_count
    local_rows = tmatrix.shape[0]
    table = shell_tables(contrast.shape[1] // 2)
    arranged = arrange_contrast(contrast, table)
    position = np.argsort(np.array(order))
    distance = (jnp.asarray(position, jnp.int32) - jnp.asarray(position, jnp.int32)[mine_row]) % row_count
    scalars = jnp.concatenate([jnp.asarray(table["offsets"]), distance, mine_col[None].astype(jnp.int32)])

    def around(value, hops):
        pairs = [(order[i], order[(i + hops) % row_count]) for i in range(row_count)]
        return lax.ppermute(value, "row", pairs)

    def across(value, flip):
        return lax.ppermute(value, "col", [(i, i ^ flip) for i in range(col_count)])

    def scatter(block):
        product = lax.dot_general(
            block.reshape(-1, depth), tmatrix, (((1,), (1,)), ((), ())), preferred_element_type=jnp.float32
        ).astype(jnp.bfloat16)
        product = product.reshape(block.shape[:-1] + (local_rows,))
        total = product[:, 0].astype(jnp.float32)
        for flip in range(1, col_count):
            total = total + across(product[:, flip], flip).astype(jnp.float32)
        return total.astype(jnp.bfloat16)

    turned = panel.T.reshape(col_count, per_device, depth)
    start = jnp.stack([lax.dynamic_index_in_dim(turned, mine_col ^ j, 0, keepdims=False) for j in range(col_count)])
    current = start
    for iteration in range(ITERS):
        held = [None] * row_count
        held[0] = scatter(current[None])[0]
        ahead = behind = current
        for hop in range(1, (row_count - 1) // 2 + 1):
            ahead, behind = around(ahead, 1), around(behind, -1)
            sums = scatter(jnp.stack([ahead, behind]))
            held[row_count - hop] = around(sums[1], hop)
            held[hop] = around(sums[0], -hop)
        if row_count % 2 == 0:
            cut = per_device // 2
            ahead, behind = around(ahead[:, :cut], 1), around(behind[:, cut:], -1)
            sums = scatter(jnp.concatenate([ahead, behind], axis=1)[None])[0]
            held[row_count // 2] = around(sums, row_count // 2)
        coupled = couple(scalars, jnp.stack(held), arranged, table, col_count)
        pieces = [coupled[0]] + [across(coupled[j], j) for j in range(1, col_count)]
        current = (start.astype(jnp.float32) + jnp.stack(pieces).astype(jnp.float32)).astype(jnp.bfloat16)
    result = jnp.stack([lax.dynamic_index_in_dim(current, mine_col ^ j, 0, keepdims=False) for j in range(col_count)])
    return result.reshape(width, depth).T


def solution(mesh):
    placed = (P("row", "col"), P("col", "row"), P())
    return jax.shard_map(
        functools.partial(body, ring_of(mesh)),
        mesh=mesh, in_specs=placed, out_specs=P("col", "row"), check_vma=False,
    )
```
